32 devices in a mesh: site: 16 (over z, x, core), fsdp: 2 (over y).
Axes of the slice: x: 2, y: 2, z: 4, core: 2. Of those that a mesh axis runs over, the one named last changes fastest.
Arguments:
- tokens: bfloat16 [4096, 5120], P(('site', 'fsdp')), may hold values from -6 to 6
- norm_gain: float32 [5120], replicated, may hold values from 0.1 to 1.9
- state: bfloat16 [16, 5120, 1024], P('site', 'fsdp'), may hold values from -6 to 6
- weight_sum: float32 [16], P('site'), may hold values from 0.5 to 2
- key_value_grad: bfloat16 [4096, 1024], P(('site', 'fsdp')), may hold values from -6 to 6
- round_number: int32 [1], replicated, may hold values from 0 to 1048575
Outputs:
- projected: bfloat16 [4096, 1024], P(('site', 'fsdp'))
- new_state: bfloat16 [16, 5120, 1024], P('site', 'fsdp')
- new_weight: float32 [16], P('site')
The draws below stay inside these ranges and needn't reach their ends.
Inputs may be any that keep to these rules, and one draw needn't show every extreme that they name: With k = round_number mod 4, site s pushes to site (s + 2^k) mod 16.
All inputs are finite; a program needn't handle non-finite values.
Results may differ from the reference program's by a relative error of at most 0.0058.
Values may be sent and summed in bfloat16 or wider, within the bound.
A program may use at most 128 MiB of HBM per device.

```python
import math
import jax
import jax.numpy as jnp
from jax import lax

D = 5120
KMAX = 4
KVW = 1024
SITES = 16
SITE_TOKENS = 256
TOKENS = 4096


def level_of(key, extent, pieces, least, high):
    def one(position, blocks):
        steps = jax.random.uniform(jax.random.fold_in(jax.random.fold_in(key, 6), position), (blocks,), jnp.float32, least / len(pieces), high / len(pieces))
        return jnp.repeat(jnp.exp(steps), extent[position] // blocks).reshape((-1,) + (1,) * (len(extent) - position - 1))

    loudness = one(*pieces[0])
    for cut in pieces[1:]:
        loudness = loudness * one(*cut)
    return loudness


def normal_values(stream_key, dims, scale, reach, pieces=(), kind=jnp.bfloat16):
    drawn = jax.random.normal(stream_key, dims, jnp.float32) * scale
    if len(pieces) > 0:
        drawn = level_of(stream_key, dims, pieces, -0.22, 0.18) * drawn
    return jnp.clip(drawn, min=-reach, max=reach).astype(kind)


def setup_inputs(seed: int = 0) -> dict:
    arg_keys = jax.random.split(jax.random.key(seed), 7)
    return {
        "tokens": normal_values(arg_keys[0], (TOKENS, D), 1.0, 6.0, ((0, 32),)),
        "norm_gain": jnp.clip(1.0 + 0.18 * jax.random.normal(arg_keys[1], (D,), jnp.float32), 0.1, 1.9),
        "state": normal_values(arg_keys[2], (SITES, D, KVW), 1.0, 6.0, ((0, 16), (1, 2))),
        "weight_sum": jnp.clip(jnp.exp(math.log(2.0) - 1.3862944 * jax.random.uniform(arg_keys[3], (SITES,), jnp.float32) ** level_of(arg_keys[3], (SITES,), ((0, 16),), -0.2, 0.2)), 0.5, 2.0),
        "key_value_grad": normal_values(arg_keys[4], (TOKENS, KVW), 1.0, 6.0, ((0, 32),)),
        "round_number": jax.random.randint(arg_keys[5], (1,), 0, 1048576).astype(jnp.int32),
    }


def reference(tokens, norm_gain, state, weight_sum, key_value_grad, round_number):
    factor = D ** (-0.5)
    site_tokens = tokens.reshape(SITES, SITE_TOKENS, D)
    site_grads = key_value_grad.reshape(SITES, SITE_TOKENS, KVW)

    def one_site(operands):
        block_tokens, stored, weight, cotangent = operands
        values = block_tokens.astype(jnp.float32)
        inverse = lax.rsqrt(lax.optimization_barrier(jnp.mean(values * values, axis=1, keepdims=True)) + 1e-06)
        normed = (values * inverse * norm_gain).astype(jnp.bfloat16)
        debiased = (stored.astype(jnp.float32) / weight).astype(jnp.bfloat16)
        keys = (jnp.dot(normed, debiased, preferred_element_type=jnp.float32) * factor).astype(jnp.bfloat16)
        gradient = jnp.dot(normed.T, cotangent, preferred_element_type=jnp.float32) * factor
        stepped = stored.astype(jnp.float32) - gradient
        return (keys, stepped)
    keys, stepped = lax.map(one_site, (site_tokens, state, weight_sum, site_grads))
    exponent = jnp.remainder(round_number[0].astype(jnp.int32), jnp.int32(KMAX))
    offset = jnp.left_shift(jnp.int32(1), exponent)
    moved = jnp.roll(stepped, offset, axis=0)
    new_state = (0.5 * (stepped + moved)).astype(jnp.bfloat16)
    new_weight = 0.5 * (weight_sum + jnp.roll(weight_sum, offset, axis=0))
    return (keys.reshape(TOKENS, KVW), new_state, new_weight)
```

```python
from functools import partial

import jax
import jax.numpy as jnp
from jax import lax
from jax.experimental import pallas as pl
from jax.experimental.pallas import tpu as pltpu
from jax.sharding import PartitionSpec as P

KMAX = 4
C = 128
F32, BF16 = jnp.float32, jnp.bfloat16


def kernel(
    offset, sites, shards, factor,
    tokens, gain, state, weight, grads,
    projected, renewed, new_weight,
    tok, gall, cols, nsend, inv, held, own, push, landed, out, acc, terms, outp, wsend, wland,
    load_sem, gsend_sem, grecv_sem, csend_sem, crecv_sem, st_sem, psend_sem, precv_sem,
    out_sem, tsend_sem, trecv_sem, w_sem, outp_sem,
):
    chunks, _, width = held.shape
    rows, features = tok.shape
    block = chunks * C
    me = lax.axis_index("fsdp")
    site = lax.axis_index("site")
    ahead = lax.rem(site + offset, sites)
    behind = lax.rem(site + (sites - offset), sites)
    mine = pl.ds(pl.multiple_of(me * rows, rows), rows)

    def peer(j):
        return lax.rem(me + j, shards)

    def remote(src, dst, send, recv, device):
        return pltpu.make_async_remote_copy(
            src_ref=src, dst_ref=dst, send_sem=send, recv_sem=recv,
            device_id=device, device_id_type=pl.DeviceIdType.MESH,
        )

    def grad_copy(j):
        return remote(grads, gall.at[mine], gsend_sem.at[j - 1], grecv_sem.at[j - 1], {"fsdp": peer(j)})

    def cols_copy(j, c):
        return remote(
            nsend.at[j - 1, c], cols.at[c, mine], csend_sem.at[j - 1, c], crecv_sem.at[j - 1, c],
            {"fsdp": peer(j)},
        )

    def push_copy(c):
        return remote(push.at[c], landed.at[c], psend_sem.at[c], precv_sem.at[c], {"site": ahead})

    def terms_copy(j):
        theirs = pl.ds(pl.multiple_of(peer(j) * rows, rows), rows)
        return remote(
            acc.at[theirs], terms.at[j - 1], tsend_sem.at[j - 1], trecv_sem.at[j - 1], {"fsdp": peer(j)}
        )

    def weight_copy():
        return remote(wsend, wland, w_sem.at[0], w_sem.at[1], {"site": ahead})

    def chunk_rows(c):
        return pl.ds(pl.multiple_of(c * C, C), C)

    def held_copy(c):
        return pltpu.make_async_copy(state.at[0, chunk_rows(c)], held.at[c], st_sem.at[c])

    def out_copy(c):
        return pltpu.make_async_copy(out.at[c], renewed.at[0, chunk_rows(c)], out_sem.at[c])

    tok_load = pltpu.make_async_copy(tokens, tok, load_sem.at[0])
    grad_load = pltpu.make_async_copy(grads, gall.at[mine], load_sem.at[1])
    tok_load.start()
    grad_load.start()

    barrier = pltpu.get_barrier_semaphore()
    for j in range(1, shards):
        pl.semaphore_signal(
            barrier, inc=1, device_id={"fsdp": peer(j)}, device_id_type=pl.DeviceIdType.MESH
        )
    for other in (ahead, behind):
        pl.semaphore_signal(
            barrier, inc=1, device_id={"site": other}, device_id_type=pl.DeviceIdType.MESH
        )
    pl.semaphore_wait(barrier, shards + 1)

    for j in range(1, shards):
        grad_copy(j).start()

    @pl.loop(0, chunks)
    def _(c):
        held_copy(c).start()

    w = weight[0]
    wsend[...] = jnp.full(wsend.shape, w, F32)
    weight_copy().start()

    tok_load.wait()

    def squares(i, total):
        v = tok[:, pl.ds(pl.multiple_of(i * 128, 128), 128)].astype(F32)
        return total + v * v

    total = lax.fori_loop(0, features // 128, squares, jnp.zeros((rows, 128), F32))
    mean = jnp.sum(total, axis=1, keepdims=True) * (1.0 / features)
    inv[...] = jnp.broadcast_to(lax.rsqrt(mean + 1e-06), inv.shape)

    def piece(p, c):
        at = pl.ds(pl.multiple_of(p * block + c * C, C), C)
        return (tok[:, at].astype(F32) * inv[...] * gain[:, at]).astype(BF16)

    @pl.loop(0, chunks)
    def _(c):
        for j in range(1, shards):
            nsend[j - 1, c] = piece(peer(j), c)
            cols_copy(j, c).start()

    @pl.loop(0, chunks)
    def _(c):
        cols[c, mine] = piece(me, c)

    grad_load.wait()
    for j in range(1, shards):
        grad_copy(j).wait_recv()

    @pl.loop(0, chunks)
    def _(c):
        held_copy(c).wait()
        for j in range(1, shards):
            cols_copy(j, c).wait_recv()
        gradient = lax.dot_general(
            cols[c], gall[...], (((0,), (0,)), ((), ())), preferred_element_type=F32
        )
        stepped = held[c].astype(F32) - gradient * factor
        own[c] = stepped
        push[c] = stepped.astype(BF16)
        push_copy(c).start()

    acc[...] = jnp.zeros_like(acc)

    @pl.loop(0, chunks)
    def _(c):
        debiased = (held[c].astype(F32) / w).astype(BF16)
        acc[...] += jnp.dot(cols[c], debiased, preferred_element_type=F32)

    for j in range(1, shards):
        terms_copy(j).start()
    for j in range(1, shards):
        terms_copy(j).wait_recv()
    total = acc[mine]
    for j in range(1, shards):
        total = total + terms[j - 1]
    outp[...] = (total * factor).astype(BF16)
    outp_copy = pltpu.make_async_copy(outp, projected, outp_sem.at[0])
    outp_copy.start()

    @pl.loop(0, chunks)
    def _(c):
        push_copy(c).wait_recv()
        out[c] = (0.5 * (own[c] + landed[c].astype(F32))).astype(BF16)
        out_copy(c).start()

    weight_copy().wait()
    new_weight[0] = 0.5 * (w + jnp.max(wland[...]))

    for j in range(1, shards):
        grad_copy(j).wait_send()
        terms_copy(j).wait_send()
    outp_copy.wait()

    @pl.loop(0, chunks)
    def _(c):
        for j in range(1, shards):
            cols_copy(j, c).wait_send()
        push_copy(c).wait_send()
        out_copy(c).wait()


def round_with(offset_index, sites, shards, tokens, norm_gain, state, weight_sum, grads):
    rows, features = tokens.shape
    _, block, width = state.shape
    chunks = block // C
    others = max(shards - 1, 1)
    dma = pltpu.SemaphoreType.DMA
    anywhere = pl.BlockSpec(memory_space=pl.ANY)
    vmem = pl.BlockSpec(memory_space=pltpu.VMEM)
    smem = pl.BlockSpec(memory_space=pltpu.SMEM)
    return pl.pallas_call(
        partial(kernel, 2**offset_index, sites, shards, features ** (-0.5)),
        out_shape=(
            jax.ShapeDtypeStruct((rows, width), BF16),
            jax.ShapeDtypeStruct(state.shape, BF16),
            jax.ShapeDtypeStruct((1,), F32),
        ),
        in_specs=[anywhere, vmem, anywhere, smem, anywhere],
        out_specs=(anywhere, anywhere, smem),
        scratch_shapes=[
            pltpu.VMEM((rows, features), BF16),
            pltpu.VMEM((shards * rows, width), BF16),
            pltpu.VMEM((chunks, shards * rows, C), BF16),
            pltpu.VMEM((others, chunks, rows, C), BF16),
            pltpu.VMEM((rows, C), F32),
            pltpu.VMEM((chunks, C, width), BF16),
            pltpu.VMEM((chunks, C, width), F32),
            pltpu.VMEM((chunks, C, width), BF16),
            pltpu.VMEM((chunks, C, width), BF16),
            pltpu.VMEM((chunks, C, width), BF16),
            pltpu.VMEM((shards * rows, width), F32),
            pltpu.VMEM((others, rows, width), F32),
            pltpu.VMEM((rows, width), BF16),
            pltpu.VMEM((8, 128), F32),
            pltpu.VMEM((8, 128), F32),
            dma((2,)),
            dma((others,)),
            dma((others,)),
            dma((others, chunks)),
            dma((others, chunks)),
            dma((chunks,)),
            dma((chunks,)),
            dma((chunks,)),
            dma((chunks,)),
            dma((others,)),
            dma((others,)),
            dma((2,)),
            dma((1,)),
        ],
        compiler_params=pltpu.CompilerParams(
            collective_id=offset_index, has_side_effects=True, vmem_limit_bytes=56 * 2**20
        ),
        name=f"round_{offset_index}",
    )(tokens, norm_gain, state, weight_sum, grads)


def solution(mesh):
    sites, shards = mesh.shape["site"], mesh.shape["fsdp"]

    def body(tokens, norm_gain, state, weight_sum, key_value_grad, round_number):
        branches = [partial(round_with, k, sites, shards) for k in range(KMAX)]
        which = jnp.remainder(round_number[0], jnp.int32(KMAX))
        return lax.switch(
            which, branches, tokens, norm_gain.reshape(1, -1), state, weight_sum, key_value_grad
        )

    tokens_spec = P(("site", "fsdp"), None)
    state_spec = P("site", "fsdp", None)
    return jax.shard_map(
        body,
        mesh=mesh,
        in_specs=(tokens_spec, P(), state_spec, P("site"), tokens_spec, P()),
        out_specs=(tokens_spec, state_spec, P("site")),
        check_vma=False,
    )
```

```python
from functools import partial

import jax
import jax.numpy as jnp
from jax import lax
from jax.experimental import pallas as pl
from jax.experimental.pallas import tpu as pltpu
from jax.sharding import PartitionSpec as P

KMAX = 4
GROUPS = 4
LEAD = 2
F32, BF16 = jnp.float32, jnp.bfloat16


def kernel(
    offset, sites, shards, factor,
    tokens, gain, state, weight, grads,
    projected, renewed, new_weight,
    tok, gall, cols, nsend, inv, held, own, push, landed, acc, terms, wsend, wland,
    load_sem, gsend_sem, grecv_sem, csend_sem, crecv_sem, st_sem, psend_sem, precv_sem,
    tsend_sem, trecv_sem, w_sem,
):
    chunks, C, width = held.shape
    rows, features = tok.shape
    block = chunks * C
    part = width // GROUPS
    me = lax.axis_index("fsdp")
    site = lax.axis_index("site")
    ahead = lax.rem(site + offset, sites)
    behind = lax.rem(site + (sites - offset), sites)
    mine = pl.ds(pl.multiple_of(me * rows, rows), rows)

    def peer(j):
        return lax.rem(me + j, shards)

    def remote(src, dst, send, recv, device):
        return pltpu.make_async_remote_copy(
            src_ref=src, dst_ref=dst, send_sem=send, recv_sem=recv,
            device_id=device, device_id_type=pl.DeviceIdType.MESH,
        )

    def group(q):
        return pl.ds(pl.multiple_of(q * part, part), part)

    def grad_copy(j, q):
        return remote(
            grads.at[:, group(q)], gall.at[q, mine], gsend_sem.at[j - 1, q], grecv_sem.at[j - 1, q],
            {"fsdp": peer(j)},
        )

    def grad_load(q):
        return pltpu.make_async_copy(grads.at[:, group(q)], gall.at[q, mine], load_sem.at[1 + q])

    def cols_copy(j, c):
        return remote(
            nsend.at[j - 1, c], cols.at[c, mine], csend_sem.at[j - 1, c], crecv_sem.at[j - 1, c],
            {"fsdp": peer(j)},
        )

    def push_copy(u):
        return remote(push.at[u], landed.at[u], psend_sem.at[u], precv_sem.at[u], {"site": ahead})

    def terms_copy(j):
        theirs = pl.ds(pl.multiple_of(peer(j) * rows, rows), rows)
        return remote(
            acc.at[theirs], terms.at[j - 1], tsend_sem.at[j - 1], trecv_sem.at[j - 1], {"fsdp": peer(j)}
        )

    def weight_copy():
        return remote(wsend, wland, w_sem.at[0], w_sem.at[1], {"site": ahead})

    def chunk_rows(c):
        return pl.ds(pl.multiple_of(c * C, C), C)

    def held_copy(c):
        return pltpu.make_async_copy(state.at[0, chunk_rows(c)], held.at[c], st_sem.at[c])

    tok_load = pltpu.make_async_copy(tokens, tok, load_sem.at[0])
    tok_load.start()
    for q in range(GROUPS):
        grad_load(q).start()

    barrier = pltpu.get_barrier_semaphore()
    for j in range(1, shards):
        pl.semaphore_signal(
            barrier, inc=1, device_id={"fsdp": peer(j)}, device_id_type=pl.DeviceIdType.MESH
        )
    for other in (ahead, behind):
        pl.semaphore_signal(
            barrier, inc=1, device_id={"site": other}, device_id_type=pl.DeviceIdType.MESH
        )

    @pl.loop(0, chunks)
    def _(c):
        held_copy(c).start()

    w = weight[0]
    wsend[...] = jnp.full(wsend.shape, w, F32)
    tok_load.wait()

    def squares(i, total):
        v = tok[:, pl.ds(pl.multiple_of(i * 128, 128), 128)].astype(F32)
        return total + v * v

    total = lax.fori_loop(0, features // 128, squares, jnp.zeros((rows, 128), F32), unroll=4)
    mean = jnp.sum(total, axis=1, keepdims=True) * (1.0 / features)
    inv[...] = jnp.broadcast_to(lax.rsqrt(mean + 1e-06), inv.shape)

    def piece(p, c):
        at = pl.ds(pl.multiple_of(p * block + c * C, C), C)
        return (tok[:, at].astype(F32) * inv[...] * gain[:, at]).astype(BF16)

    def send_pieces(c):
        for j in range(1, shards):
            nsend[j - 1, c] = piece(peer(j), c)
            cols_copy(j, c).start()

    def send_grads(q):
        for j in range(1, shards):
            grad_copy(j, q).start()

    for j in range(1, shards):
        nsend[j - 1, 0] = piece(peer(j), 0)
    pl.semaphore_wait(barrier, shards + 1)
    send_grads(0)
    for j in range(1, shards):
        cols_copy(j, 0).start()
    for q in range(1, LEAD + 1):
        send_grads(q)

    def step(q, c):
        u = c * GROUPS + q
        gradient = lax.dot_general(
            cols[c], gall[q], (((0,), (0,)), ((), ())), preferred_element_type=F32
        )
        stepped = held[c, :, group(q)].astype(F32) - gradient * factor
        own[u] = stepped
        push[u] = stepped.astype(BF16)
        push_copy(u).start()

    def grads_here(q):
        grad_load(q).wait()
        for j in range(1, shards):
            grad_copy(j, q).wait_recv()

    cols[0, mine] = piece(me, 0)
    held_copy(0).wait()
    for j in range(1, shards):
        cols_copy(j, 0).wait_recv()
    for q in range(GROUPS):
        grads_here(q)
        step(q, 0)
        if q + LEAD + 1 < GROUPS:
            send_grads(q + LEAD + 1)
        elif q + LEAD + 1 - GROUPS < LEAD:
            send_pieces(q + LEAD + 2 - GROUPS)
    weight_copy().start()

    @pl.loop(1, chunks)
    def _(c):
        @pl.when(c + LEAD < chunks)
        def _():
            send_pieces(c + LEAD)

        cols[c, mine] = piece(me, c)
        held_copy(c).wait()
        for j in range(1, shards):
            cols_copy(j, c).wait_recv()
        for q in range(GROUPS):
            step(q, c)

    acc[...] = jnp.zeros_like(acc)

    @pl.loop(0, chunks)
    def _(c):
        debiased = (held[c].astype(F32) / w).astype(BF16)
        acc[...] += jnp.dot(cols[c], debiased, preferred_element_type=F32)

    for j in range(1, shards):
        terms_copy(j).start()
    for j in range(1, shards):
        terms_copy(j).wait_recv()
    total = acc[mine]
    for j in range(1, shards):
        total = total + terms[j - 1]
    projected[...] = (total * factor).astype(BF16)

    @pl.loop(0, chunks)
    def _(c):
        for q in range(GROUPS):
            u = c * GROUPS + q
            push_copy(u).wait_recv()
            mixed = 0.5 * (own[u] + landed[u].astype(F32))
            renewed[0, chunk_rows(c), group(q)] = mixed.astype(BF16)

    weight_copy().wait()
    new_weight[0] = 0.5 * (w + jnp.max(wland[...]))

    for j in range(1, shards):
        terms_copy(j).wait_send()
        for q in range(GROUPS):
            grad_copy(j, q).wait_send()

    @pl.loop(0, chunks)
    def _(c):
        for j in range(1, shards):
            cols_copy(j, c).wait_send()

    @pl.loop(0, GROUPS * chunks)
    def _(u):
        push_copy(u).wait_send()


def store(projected, renewed, projected_out, renewed_out, sem):
    copies = [
        pltpu.make_async_copy(renewed, renewed_out, sem.at[0]),
        pltpu.make_async_copy(projected, projected_out, sem.at[1]),
    ]
    for copy in copies:
        copy.start()
    for copy in copies:
        copy.wait()


def round_with(offset_index, sites, shards, tokens, norm_gain, state, weight_sum, grads):
    rows, features = tokens.shape
    _, block, width = state.shape
    C = 256 if block % 256 == 0 else 128
    chunks, part = block // C, width // GROUPS
    others = max(shards - 1, 1)
    dma = pltpu.SemaphoreType.DMA
    anywhere = pl.BlockSpec(memory_space=pl.ANY)
    vmem = pl.BlockSpec(memory_space=pltpu.VMEM)
    smem = pl.BlockSpec(memory_space=pltpu.SMEM)
    projected, renewed, new_weight = pl.pallas_call(
        partial(kernel, 2**offset_index, sites, shards, features ** (-0.5)),
        out_shape=(
            pltpu.VMEM((rows, width), BF16),
            pltpu.VMEM(state.shape, BF16),
            jax.ShapeDtypeStruct((1,), F32),
        ),
        in_specs=[anywhere, vmem, anywhere, smem, anywhere],
        out_specs=(vmem, vmem, smem),
        scratch_shapes=[
            pltpu.VMEM((rows, features), BF16),
            pltpu.VMEM((GROUPS, shards * rows, part), BF16),
            pltpu.VMEM((chunks, shards * rows, C), BF16),
            pltpu.VMEM((others, chunks, rows, C), BF16),
            pltpu.VMEM((rows, C), F32),
            pltpu.VMEM((chunks, C, width), BF16),
            pltpu.VMEM((GROUPS * chunks, C, part), F32),
            pltpu.VMEM((GROUPS * chunks, C, part), BF16),
            pltpu.VMEM((GROUPS * chunks, C, part), BF16),
            pltpu.VMEM((shards * rows, width), F32),
            pltpu.VMEM((others, rows, width), F32),
            pltpu.VMEM((8, 128), F32),
            pltpu.VMEM((8, 128), F32),
            dma((1 + GROUPS,)),
            dma((others, GROUPS)),
            dma((others, GROUPS)),
            dma((others, chunks)),
            dma((others, chunks)),
            dma((chunks,)),
            dma((GROUPS * chunks,)),
            dma((GROUPS * chunks,)),
            dma((others,)),
            dma((others,)),
            dma((2,)),
        ],
        compiler_params=pltpu.CompilerParams(
            collective_id=offset_index, has_side_effects=True, vmem_limit_bytes=48 * 2**20
        ),
        name=f"round_{offset_index}",
    )(tokens, norm_gain, state, weight_sum, grads)
    projected, renewed = pl.pallas_call(
        store,
        out_shape=(
            jax.ShapeDtypeStruct((rows, width), BF16),
            jax.ShapeDtypeStruct(state.shape, BF16),
        ),
        in_specs=[anywhere, anywhere],
        out_specs=(anywhere, anywhere),
        scratch_shapes=[dma((2,))],
        compiler_params=pltpu.CompilerParams(vmem_limit_bytes=2**20),
        name=f"store_{offset_index}",
    )(projected, renewed)
    return projected, renewed, new_weight


def solution(mesh):
    sites, shards = mesh.shape["site"], mesh.shape["fsdp"]

    def body(tokens, norm_gain, state, weight_sum, key_value_grad, round_number):
        branches = [partial(round_with, k, sites, shards) for k in range(KMAX)]
        which = jnp.remainder(round_number[0], jnp.int32(KMAX))
        return lax.switch(
            which, branches, tokens, norm_gain.reshape(1, -1), state, weight_sum, key_value_grad
        )

    tokens_spec = P(("site", "fsdp"), None)
    state_spec = P("site", "fsdp", None)
    return jax.shard_map(
        body,
        mesh=mesh,
        in_specs=(tokens_spec, P(), state_spec, P("site"), tokens_spec, P()),
        out_specs=(tokens_spec, state_spec, P("site")),
        check_vma=False,
    )
```

```python
from functools import partial

import jax
import jax.numpy as jnp
from jax import lax
from jax.experimental import pallas as pl
from jax.experimental.pallas import tpu as pltpu
from jax.sharding import PartitionSpec as P

KMAX = 4
GROUPS = 4
LEAD = 2
PARTS = 4
F32, BF16 = jnp.float32, jnp.bfloat16


def kernel(
    offset, sites, shards, factor,
    tokens, gain, state, weight, grads,
    projected, renewed, new_weight,
    tok, gall, cols, nsend, inv, held, own, push, landed, acc, terms, wsend, wland,
    load_sem, gsend_sem, grecv_sem, csend_sem, crecv_sem, st_sem, psend_sem, precv_sem,
    tsend_sem, trecv_sem, w_sem,
):
    chunks, C, width = held.shape
    rows, features = tok.shape
    block = chunks * C
    part = width // GROUPS
    me = lax.axis_index("fsdp")
    site = lax.axis_index("site")
    ahead = lax.rem(site + offset, sites)
    behind = lax.rem(site + (sites - offset), sites)
    mine = pl.ds(pl.multiple_of(me * rows, rows), rows)

    def peer(j):
        return lax.rem(me + j, shards)

    def remote(src, dst, send, recv, device):
        return pltpu.make_async_remote_copy(
            src_ref=src, dst_ref=dst, send_sem=send, recv_sem=recv,
            device_id=device, device_id_type=pl.DeviceIdType.MESH,
        )

    def group(q):
        return pl.ds(pl.multiple_of(q * part, part), part)

    def grad_copy(j, q):
        return remote(
            grads.at[:, group(q)], gall.at[q, mine], gsend_sem.at[j - 1, q], grecv_sem.at[j - 1, q],
            {"fsdp": peer(j)},
        )

    def grad_load(q):
        return pltpu.make_async_copy(grads.at[:, group(q)], gall.at[q, mine], load_sem.at[1 + q])

    def cols_copy(j, c):
        return remote(
            nsend.at[j - 1, c], cols.at[c, mine], csend_sem.at[j - 1, c], crecv_sem.at[j - 1, c],
            {"fsdp": peer(j)},
        )

    def push_copy(u):
        return remote(push.at[u], landed.at[u], psend_sem.at[u], precv_sem.at[u], {"site": ahead})

    def terms_copy(j):
        theirs = pl.ds(pl.multiple_of(peer(j) * rows, rows), rows)
        return remote(
            acc.at[theirs], terms.at[j - 1], tsend_sem.at[j - 1], trecv_sem.at[j - 1], {"fsdp": peer(j)}
        )

    def weight_copy():
        return remote(wsend, wland, w_sem.at[0], w_sem.at[1], {"site": ahead})

    def chunk_rows(c):
        return pl.ds(pl.multiple_of(c * C, C), C)

    def held_copy(c):
        return pltpu.make_async_copy(state.at[0, chunk_rows(c)], held.at[c], st_sem.at[c])

    tok_load = pltpu.make_async_copy(tokens, tok, load_sem.at[0])
    tok_load.start()
    for q in range(GROUPS):
        grad_load(q).start()

    barrier = pltpu.get_barrier_semaphore()
    for j in range(1, shards):
        pl.semaphore_signal(
            barrier, inc=1, device_id={"fsdp": peer(j)}, device_id_type=pl.DeviceIdType.MESH
        )
    for other in (ahead, behind):
        pl.semaphore_signal(
            barrier, inc=1, device_id={"site": other}, device_id_type=pl.DeviceIdType.MESH
        )

    def send_grads(q):
        for j in range(1, shards):
            grad_copy(j, q).start()

    pl.semaphore_wait(barrier, shards + 1)
    send_grads(0)

    @pl.loop(0, chunks)
    def _(c):
        held_copy(c).start()

    w = weight[0]
    wsend[...] = jnp.full(wsend.shape, w, F32)
    tok_load.wait()

    def squares(i, total):
        v = tok[:, pl.ds(pl.multiple_of(i * 128, 128), 128)].astype(F32)
        return total + v * v

    total = lax.fori_loop(0, features // 128, squares, jnp.zeros((rows, 128), F32), unroll=4)
    mean = jnp.sum(total, axis=1, keepdims=True) * (1.0 / features)
    inv[...] = jnp.broadcast_to(lax.rsqrt(mean + 1e-06), inv.shape)

    def piece(p, c):
        at = pl.ds(pl.multiple_of(p * block + c * C, C), C)
        return (tok[:, at].astype(F32) * inv[...] * gain[:, at]).astype(BF16)

    def send_pieces(c):
        for j in range(1, shards):
            nsend[j - 1, c] = piece(peer(j), c)
            cols_copy(j, c).start()

    for j in range(1, shards):
        nsend[j - 1, 0] = piece(peer(j), 0)
    for j in range(1, shards):
        cols_copy(j, 0).start()
    for q in range(1, LEAD + 1):
        send_grads(q)

    def step(q, c):
        u = c * GROUPS + q
        gradient = lax.dot_general(
            cols[c], gall[q], (((0,), (0,)), ((), ())), preferred_element_type=F32
        )
        stepped = held[c, :, group(q)].astype(F32) - gradient * factor
        own[u] = stepped
        push[u] = stepped.astype(BF16)
        push_copy(u).start()

    def grads_here(q):
        grad_load(q).wait()
        for j in range(1, shards):
            grad_copy(j, q).wait_recv()

    cols[0, mine] = piece(me, 0)
    held_copy(0).wait()
    for j in range(1, shards):
        cols_copy(j, 0).wait_recv()
    for q in range(GROUPS):
        grads_here(q)
        step(q, 0)
        if q + LEAD + 1 < GROUPS:
            send_grads(q + LEAD + 1)
        elif q + LEAD + 1 - GROUPS < LEAD:
            send_pieces(q + LEAD + 2 - GROUPS)
    weight_copy().start()

    @pl.loop(1, chunks)
    def _(c):
        @pl.when(c + LEAD < chunks)
        def _():
            send_pieces(c + LEAD)

        cols[c, mine] = piece(me, c)
        held_copy(c).wait()
        for j in range(1, shards):
            cols_copy(j, c).wait_recv()
        for q in range(GROUPS):
            step(q, c)

    acc[...] = jnp.zeros_like(acc)

    @pl.loop(0, chunks)
    def _(c):
        debiased = (held[c].astype(F32) / w).astype(BF16)
        acc[...] += jnp.dot(cols[c], debiased, preferred_element_type=F32)

    for j in range(1, shards):
        terms_copy(j).start()
    for j in range(1, shards):
        terms_copy(j).wait_recv()
    total = acc[mine]
    for j in range(1, shards):
        total = total + terms[j - 1]
    projected[...] = (total * factor).astype(BF16)

    @pl.loop(0, chunks)
    def _(c):
        for q in range(GROUPS):
            u = c * GROUPS + q
            push_copy(u).wait_recv()
            mixed = 0.5 * (own[u] + landed[u].astype(F32))
            renewed[0, chunk_rows(c), group(q)] = mixed.astype(BF16)

    weight_copy().wait()
    new_weight[0] = 0.5 * (w + jnp.max(wland[...]))

    for j in range(1, shards):
        terms_copy(j).wait_send()
        for q in range(GROUPS):
            grad_copy(j, q).wait_send()

    @pl.loop(0, chunks)
    def _(c):
        for j in range(1, shards):
            cols_copy(j, c).wait_send()

    @pl.loop(0, GROUPS * chunks)
    def _(u):
        push_copy(u).wait_send()


def store(projected, renewed, projected_out, renewed_out, sem):
    rows = renewed.shape[1] // PARTS
    copies = [pltpu.make_async_copy(projected, projected_out, sem.at[PARTS])]
    for i in range(PARTS):
        at = pl.ds(i * rows, rows)
        copies.append(pltpu.make_async_copy(renewed.at[:, at], renewed_out.at[:, at], sem.at[i]))
    for copy in copies:
        copy.start()
    for copy in copies:
        copy.wait()


def round_with(offset_index, sites, shards, tokens, norm_gain, state, weight_sum, grads):
    rows, features = tokens.shape
    _, block, width = state.shape
    C = 256 if block % 256 == 0 else 128
    chunks, part = block // C, width // GROUPS
    others = max(shards - 1, 1)
    dma = pltpu.SemaphoreType.DMA
    anywhere = pl.BlockSpec(memory_space=pl.ANY)
    vmem = pl.BlockSpec(memory_space=pltpu.VMEM)
    smem = pl.BlockSpec(memory_space=pltpu.SMEM)
    projected, renewed, new_weight = pl.pallas_call(
        partial(kernel, 2**offset_index, sites, shards, features ** (-0.5)),
        out_shape=(
            pltpu.VMEM((rows, width), BF16),
            pltpu.VMEM(state.shape, BF16),
            jax.ShapeDtypeStruct((1,), F32),
        ),
        in_specs=[anywhere, vmem, anywhere, smem, anywhere],
        out_specs=(vmem, vmem, smem),
        scratch_shapes=[
            pltpu.VMEM((rows, features), BF16),
            pltpu.VMEM((GROUPS, shards * rows, part), BF16),
            pltpu.VMEM((chunks, shards * rows, C), BF16),
            pltpu.VMEM((others, chunks, rows, C), BF16),
            pltpu.VMEM((rows, C), F32),
            pltpu.VMEM((chunks, C, width), BF16),
            pltpu.VMEM((GROUPS * chunks, C, part), F32),
            pltpu.VMEM((GROUPS * chunks, C, part), BF16),
            pltpu.VMEM((GROUPS * chunks, C, part), BF16),
            pltpu.VMEM((shards * rows, width), F32),
            pltpu.VMEM((others, rows, width), F32),
            pltpu.VMEM((8, 128), F32),
            pltpu.VMEM((8, 128), F32),
            dma((1 + GROUPS,)),
            dma((others, GROUPS)),
            dma((others, GROUPS)),
            dma((others, chunks)),
            dma((others, chunks)),
            dma((chunks,)),
            dma((GROUPS * chunks,)),
            dma((GROUPS * chunks,)),
            dma((others,)),
            dma((others,)),
            dma((2,)),
        ],
        compiler_params=pltpu.CompilerParams(
            collective_id=offset_index, has_side_effects=True, vmem_limit_bytes=48 * 2**20
        ),
        name=f"round_{offset_index}",
    )(tokens, norm_gain, state, weight_sum, grads)
    projected, renewed = pl.pallas_call(
        store,
        out_shape=(
            jax.ShapeDtypeStruct((rows, width), BF16),
            jax.ShapeDtypeStruct(state.shape, BF16),
        ),
        in_specs=[anywhere, anywhere],
        out_specs=(anywhere, anywhere),
        scratch_shapes=[dma((PARTS + 1,))],
        compiler_params=pltpu.CompilerParams(vmem_limit_bytes=2**20),
        name=f"store_{offset_index}",
    )(projected, renewed)
    return projected, renewed, new_weight


def solution(mesh):
    sites, shards = mesh.shape["site"], mesh.shape["fsdp"]

    def body(tokens, norm_gain, state, weight_sum, key_value_grad, round_number):
        branches = [partial(round_with, k, sites, shards) for k in range(KMAX)]
        which = jnp.remainder(round_number[0], jnp.int32(KMAX))
        return lax.switch(
            which, branches, tokens, norm_gain.reshape(1, -1), state, weight_sum, key_value_grad
        )

    tokens_spec = P(("site", "fsdp"), None)
    state_spec = P("site", "fsdp", None)
    return jax.shard_map(
        body,
        mesh=mesh,
        in_specs=(tokens_spec, P(), state_spec, P("site"), tokens_spec, P()),
        out_specs=(tokens_spec, state_spec, P("site")),
        check_vma=False,
    )
```

```python
from functools import partial

import jax
import jax.numpy as jnp
from jax import lax
from jax.experimental import pallas as pl
from jax.experimental.pallas import tpu as pltpu
from jax.sharding import PartitionSpec as P

KMAX = 4
GROUPS = 4
LEAD = 2
PARTS = 4
F32, BF16 = jnp.float32, jnp.bfloat16


def kernel(
    offset, sites, shards, factor,
    tokens, gains, state, weight, grads,
    projected, renewed, new_weight,
    tok, gain, gall, cols, nsend, inv, held, own, push, landed, acc, terms, wsend, wland,
    load_sem, gsend_sem, grecv_sem, csend_sem, crecv_sem, st_sem, psend_sem, precv_sem,
    tsend_sem, trecv_sem, w_sem,
):
    chunks, C, width = held.shape
    rows, features = tok.shape
    block = chunks * C
    part = width // GROUPS
    me = lax.axis_index("fsdp")
    site = lax.axis_index("site")
    ahead = lax.rem(site + offset, sites)
    behind = lax.rem(site + (sites - offset), sites)
    mine = pl.ds(pl.multiple_of(me * rows, rows), rows)

    def peer(j):
        return lax.rem(me + j, shards)

    def remote(src, dst, send, recv, device):
        return pltpu.make_async_remote_copy(
            src_ref=src, dst_ref=dst, send_sem=send, recv_sem=recv,
            device_id=device, device_id_type=pl.DeviceIdType.MESH,
        )

    def group(q):
        return pl.ds(pl.multiple_of(q * part, part), part)

    def grad_copy(j, q):
        return remote(
            grads.at[:, group(q)], gall.at[q, mine], gsend_sem.at[j - 1, q], grecv_sem.at[j - 1, q],
            {"fsdp": peer(j)},
        )

    def grad_load(q):
        return pltpu.make_async_copy(grads.at[:, group(q)], gall.at[q, mine], load_sem.at[1 + q])

    def cols_copy(j, c):
        return remote(
            nsend.at[j - 1, c], cols.at[c, mine], csend_sem.at[j - 1, c], crecv_sem.at[j - 1, c],
            {"fsdp": peer(j)},
        )

    def push_copy(u):
        return remote(push.at[u], landed.at[u], psend_sem.at[u], precv_sem.at[u], {"site": ahead})

    def terms_copy(j):
        theirs = pl.ds(pl.multiple_of(peer(j) * rows, rows), rows)
        return remote(
            acc.at[theirs], terms.at[j - 1], tsend_sem.at[j - 1], trecv_sem.at[j - 1], {"fsdp": peer(j)}
        )

    def weight_copy():
        return remote(wsend, wland, w_sem.at[0], w_sem.at[1], {"site": ahead})

    def chunk_rows(c):
        return pl.ds(pl.multiple_of(c * C, C), C)

    def held_copy(c):
        return pltpu.make_async_copy(state.at[0, chunk_rows(c)], held.at[c], st_sem.at[c])

    tok_load = pltpu.make_async_copy(tokens, tok, load_sem.at[0])
    tok_load.start()
    gain_load = pltpu.make_async_copy(gains, gain, load_sem.at[1 + GROUPS])
    gain_load.start()
    for q in range(GROUPS):
        grad_load(q).start()

    barrier = pltpu.get_barrier_semaphore()
    for j in range(1, shards):
        pl.semaphore_signal(
            barrier, inc=1, device_id={"fsdp": peer(j)}, device_id_type=pl.DeviceIdType.MESH
        )
    for other in (ahead, behind):
        pl.semaphore_signal(
            barrier, inc=1, device_id={"site": other}, device_id_type=pl.DeviceIdType.MESH
        )

    def send_grads(q):
        for j in range(1, shards):
            grad_copy(j, q).start()

    pl.semaphore_wait(barrier, shards + 1)
    send_grads(0)

    @pl.loop(0, chunks)
    def _(c):
        held_copy(c).start()

    w = weight[0]
    wsend[...] = jnp.full(wsend.shape, w, F32)
    tok_load.wait()

    def squares(i, total):
        v = tok[:, pl.ds(pl.multiple_of(i * 128, 128), 128)].astype(F32)
        return total + v * v

    total = lax.fori_loop(0, features // 128, squares, jnp.zeros((rows, 128), F32), unroll=4)
    mean = jnp.sum(total, axis=1, keepdims=True) * (1.0 / features)
    gain_load.wait()
    inv[...] = jnp.broadcast_to(lax.rsqrt(mean + 1e-06), inv.shape)

    def piece(p, c):
        at = pl.ds(pl.multiple_of(p * block + c * C, C), C)
        return (tok[:, at].astype(F32) * inv[...] * gain[:, at]).astype(BF16)

    def send_pieces(c):
        for j in range(1, shards):
            nsend[j - 1, c] = piece(peer(j), c)
            cols_copy(j, c).start()

    for j in range(1, shards):
        nsend[j - 1, 0] = piece(peer(j), 0)
    for j in range(1, shards):
        cols_copy(j, 0).start()
    for q in range(1, LEAD + 1):
        send_grads(q)

    def step(q, c):
        u = c * GROUPS + q
        gradient = lax.dot_general(
            cols[c], gall[q], (((0,), (0,)), ((), ())), preferred_element_type=F32
        )
        stepped = held[c, :, group(q)].astype(F32) - gradient * factor
        own[u] = stepped
        push[u] = stepped.astype(BF16)
        push_copy(u).start()

    def grads_here(q):
        grad_load(q).wait()
        for j in range(1, shards):
            grad_copy(j, q).wait_recv()

    cols[0, mine] = piece(me, 0)
    held_copy(0).wait()
    for j in range(1, shards):
        cols_copy(j, 0).wait_recv()
    for q in range(GROUPS):
        grads_here(q)
        step(q, 0)
        if q + LEAD + 1 < GROUPS:
            send_grads(q + LEAD + 1)
        elif q + LEAD + 1 - GROUPS < LEAD:
            send_pieces(q + LEAD + 2 - GROUPS)
    weight_copy().start()

    @pl.loop(1, chunks)
    def _(c):
        @pl.when(c + LEAD < chunks)
        def _():
            send_pieces(c + LEAD)

        cols[c, mine] = piece(me, c)
        held_copy(c).wait()
        for j in range(1, shards):
            cols_copy(j, c).wait_recv()
        for q in range(GROUPS):
            step(q, c)

    acc[...] = jnp.zeros_like(acc)

    @pl.loop(0, chunks)
    def _(c):
        debiased = (held[c].astype(F32) / w).astype(BF16)
        acc[...] += jnp.dot(cols[c], debiased, preferred_element_type=F32)

    for j in range(1, shards):
        terms_copy(j).start()
    for j in range(1, shards):
        terms_copy(j).wait_recv()
    total = acc[mine]
    for j in range(1, shards):
        total = total + terms[j - 1]
    projected[...] = (total * factor).astype(BF16)

    @pl.loop(0, chunks)
    def _(c):
        for q in range(GROUPS):
            u = c * GROUPS + q
            push_copy(u).wait_recv()
            mixed = 0.5 * (own[u] + landed[u].astype(F32))
            renewed[0, chunk_rows(c), group(q)] = mixed.astype(BF16)

    weight_copy().wait()
    new_weight[0] = 0.5 * (w + jnp.max(wland[...]))

    for j in range(1, shards):
        terms_copy(j).wait_send()
        for q in range(GROUPS):
            grad_copy(j, q).wait_send()

    @pl.loop(0, chunks)
    def _(c):
        for j in range(1, shards):
            cols_copy(j, c).wait_send()

    @pl.loop(0, GROUPS * chunks)
    def _(u):
        push_copy(u).wait_send()


def store(projected, renewed, projected_out, renewed_out, sem):
    rows = renewed.shape[1] // PARTS
    copies = [pltpu.make_async_copy(projected, projected_out, sem.at[PARTS])]
    for i in range(PARTS):
        at = pl.ds(i * rows, rows)
        copies.append(pltpu.make_async_copy(renewed.at[:, at], renewed_out.at[:, at], sem.at[i]))
    for copy in copies:
        copy.start()
    for copy in copies:
        copy.wait()


def round_with(offset_index, sites, shards, tokens, norm_gain, state, weight_sum, grads):
    rows, features = tokens.shape
    _, block, width = state.shape
    C = 256 if block % 256 == 0 else 128
    chunks, part = block // C, width // GROUPS
    others = max(shards - 1, 1)
    dma = pltpu.SemaphoreType.DMA
    anywhere = pl.BlockSpec(memory_space=pl.ANY)
    vmem = pl.BlockSpec(memory_space=pltpu.VMEM)
    smem = pl.BlockSpec(memory_space=pltpu.SMEM)
    projected, renewed, new_weight = pl.pallas_call(
        partial(kernel, 2**offset_index, sites, shards, features ** (-0.5)),
        out_shape=(
            pltpu.VMEM((rows, width), BF16),
            pltpu.VMEM(state.shape, BF16),
            jax.ShapeDtypeStruct((1,), F32),
        ),
        in_specs=[anywhere, anywhere, anywhere, smem, anywhere],
        out_specs=(vmem, vmem, smem),
        scratch_shapes=[
            pltpu.VMEM((rows, features), BF16),
            pltpu.VMEM((1, features), F32),
            pltpu.VMEM((GROUPS, shards * rows, part), BF16),
            pltpu.VMEM((chunks, shards * rows, C), BF16),
            pltpu.VMEM((others, chunks, rows, C), BF16),
            pltpu.VMEM((rows, C), F32),
            pltpu.VMEM((chunks, C, width), BF16),
            pltpu.VMEM((GROUPS * chunks, C, part), F32),
            pltpu.VMEM((GROUPS * chunks, C, part), BF16),
            pltpu.VMEM((GROUPS * chunks, C, part), BF16),
            pltpu.VMEM((shards * rows, width), F32),
            pltpu.VMEM((others, rows, width), F32),
            pltpu.VMEM((8, 128), F32),
            pltpu.VMEM((8, 128), F32),
            dma((2 + GROUPS,)),
            dma((others, GROUPS)),
            dma((others, GROUPS)),
            dma((others, chunks)),
            dma((others, chunks)),
            dma((chunks,)),
            dma((GROUPS * chunks,)),
            dma((GROUPS * chunks,)),
            dma((others,)),
            dma((others,)),
            dma((2,)),
        ],
        compiler_params=pltpu.CompilerParams(
            collective_id=offset_index, has_side_effects=True, vmem_limit_bytes=48 * 2**20
        ),
        name=f"round_{offset_index}",
    )(tokens, norm_gain, state, weight_sum, grads)
    projected, renewed = pl.pallas_call(
        store,
        out_shape=(
            jax.ShapeDtypeStruct((rows, width), BF16),
            jax.ShapeDtypeStruct(state.shape, BF16),
        ),
        in_specs=[anywhere, anywhere],
        out_specs=(anywhere, anywhere),
        scratch_shapes=[dma((PARTS + 1,))],
        compiler_params=pltpu.CompilerParams(vmem_limit_bytes=2**20),
        name=f"store_{offset_index}",
    )(projected, renewed)
    return projected, renewed, new_weight


def solution(mesh):
    sites, shards = mesh.shape["site"], mesh.shape["fsdp"]

    def body(tokens, norm_gain, state, weight_sum, key_value_grad, round_number):
        branches = [partial(round_with, k, sites, shards) for k in range(KMAX)]
        which = jnp.remainder(round_number[0], jnp.int32(KMAX))
        return lax.switch(
            which, branches, tokens, norm_gain.reshape(1, -1), state, weight_sum, key_value_grad
        )

    tokens_spec = P(("site", "fsdp"), None)
    state_spec = P("site", "fsdp", None)
    return jax.shard_map(
        body,
        mesh=mesh,
        in_specs=(tokens_spec, P(), state_spec, P("site"), tokens_spec, P()),
        out_specs=(tokens_spec, state_spec, P("site")),
        check_vma=False,
    )
```
